32 devices in a mesh: dp: 2 (over x), layer: 4 (over y, core), tensor: 4 (over z).
Axes of the slice: x: 2, y: 2, z: 4, core: 2. Of those that a mesh axis runs over, the one named last changes fastest.
Arguments:
- embeddings: bfloat16 [256, 4096], P('dp', 'tensor'), may hold values from -180 to 180
- layer_weight: bfloat16 [8, 4096, 4096], P('layer', None, 'tensor'), may hold values from -0.09375 to 0.09375
- rotation: float32 [4096, 4096], P(('dp', 'layer'), 'tensor'), may hold values from -3.2 to 3.2
Outputs:
- updated_rotation: float32 [4096, 4096], P(('dp', 'layer'), 'tensor')
The draws below stay inside these ranges and needn't reach their ends.
All inputs are finite; a program needn't handle non-finite values.
Results may differ from the reference program's by a relative error of at most 0.0042.
Values may be sent and summed in bfloat16 or wider, within the bound.
A program may use at most 128 MiB of HBM per device.

```python
import math
import jax
import jax.numpy as jnp
from jax import lax

D = 4096
TOKENS = 256
LAYERS = 8


def draw_embeddings(key, part):
    first_key, second_key = jax.random.split(key, 2)
    column = jnp.arange(D, dtype=jnp.float32) / D
    base = jnp.clip(jax.random.normal(first_key, (TOKENS, D), jnp.float32), -6.0, 6.0)
    trend = jnp.exp(math.log(10.0) * column)
    jitter = jnp.exp(jax.random.uniform(second_key, (D,), jnp.float32, 0.0, math.log(3.0)))
    return (base * (trend * jitter)[None, :]).astype(jnp.bfloat16)


def sign_parity(index):
    total = jnp.zeros((D, D), jnp.int32)
    for level in range(D.bit_length() - 1):
        row_bit = jnp.bitwise_and(jnp.right_shift(index, level), 1)
        total = total + row_bit[:, None] * row_bit[None, :]
    return total % 2


def draw_rotation(key, part):
    row_key, col_key, noise_key = jax.random.split(key, 3)
    index = jnp.arange(D, dtype=jnp.int32)
    parity = sign_parity(index)
    hadamard = (1 - 2 * parity).astype(jnp.float32)
    row_sign = (2 * jax.random.randint(row_key, (D,), 0, 2) - 1).astype(jnp.float32)
    col_sign = (2 * jax.random.randint(col_key, (D,), 0, 2) - 1).astype(jnp.float32)
    noise = 0.6 * jnp.clip(jax.random.normal(noise_key, (D, D), jnp.float32), -4.0, 4.0)
    return 0.8 * hadamard * row_sign[:, None] * col_sign[None, :] + noise


def levels(own_key, shape, cuts, least, high):
    def one(dim, shards_of):
        steps = jax.random.uniform(jax.random.fold_in(jax.random.fold_in(own_key, 6), dim), (shards_of,), jnp.float32, least / len(cuts), high / len(cuts))
        return jnp.repeat(jnp.exp(steps), shape[dim] // shards_of).reshape((-1,) + (1,) * (len(shape) - dim - 1))

    factor_of = one(*cuts[0])
    for cut in cuts[1:]:
        factor_of = factor_of * one(*cut)
    return factor_of


def scatter_about(stream_key, shape, deviation, reach, shards=(), kind=jnp.bfloat16):
    result = deviation * jax.random.normal(stream_key, shape, jnp.float32)
    if shards:
        result = result * levels(stream_key, shape, shards, -0.22, 0.18)
    return jnp.clip(result, -reach, reach).astype(kind)


def setup_inputs(seed: int = 0) -> dict:
    keys = jax.random.split(jax.random.key(seed), 4)
    embeddings = draw_embeddings(jax.random.fold_in(keys[3], 71), 0)
    layer_weight = scatter_about(keys[1], (LAYERS, D, D), D ** -0.5, 0.09375, ((0, 4), (2, 4)))
    rotation = draw_rotation(jax.random.fold_in(keys[3], 71), 0)
    return {"embeddings": embeddings, "layer_weight": layer_weight, "rotation": rotation}


def reference(embeddings, layer_weight, rotation):
    exact_mode = lax.Precision.HIGHEST
    root_width = math.sqrt(D)
    rotated = rotation / root_width
    hidden = embeddings
    gradient = jnp.zeros((D, D), jnp.float32)
    for level in range(LAYERS):
        widened = hidden.astype(jnp.float32)
        inverse = lax.rsqrt(lax.optimization_barrier(jnp.mean(widened * widened, axis=-1, keepdims=True)) + 1e-05)
        normed = (widened * inverse).astype(jnp.bfloat16)
        normed_wide = normed.astype(jnp.float32)
        projected = jnp.dot(normed_wide, rotated, precision=exact_mode)
        cubed = projected * projected * projected
        gradient = gradient + jnp.dot(normed_wide.T, cubed, precision=exact_mode)
        update = jnp.dot(normed, layer_weight[level], preferred_element_type=jnp.float32)
        hidden = (widened + update).astype(jnp.bfloat16)
    gradient = gradient / TOKENS
    cross = jnp.dot(gradient, rotated.T, precision=exact_mode)
    skew = cross - cross.T
    mean_square = jnp.mean(skew * skew)
    step_size = 0.5 / jnp.sqrt(D * (mean_square + 1e-06))
    first_product = jnp.dot(skew, rotated, precision=exact_mode)
    first_guess = rotated - step_size * first_product
    second_product = jnp.dot(skew, first_guess, precision=exact_mode)
    refined = rotated - 0.5 * step_size * (first_product + second_product)
    return root_width * refined
```

```python
import functools
import math

import jax
import jax.numpy as jnp
from jax import lax
from jax.experimental import pallas as pl
from jax.experimental.pallas import tpu as pltpu
from jax.sharding import PartitionSpec as P

ROWS = ("dp", "layer")
EVERY = ("dp", "layer", "tensor")
HALF = jnp.bfloat16
CHUNKS = 2
MESH = pl.DeviceIdType.MESH


def product(left, right, left_dim, right_dim):
    dims = (((left_dim,), (right_dim,)), ((), ()))
    return lax.dot_general(left.astype(HALF), right.astype(HALF), dims, preferred_element_type=jnp.float32)


def split(value):
    head = lax.reduce_precision(value, 8, 7)
    return head.astype(HALF), (value - head).astype(HALF)


def layers_kernel(chunks, embeddings, weight_hbm, records, hidden, outbox, weight, send_sem, recv_sem, weight_sem):
    dp, section, me = (lax.axis_index(name) for name in EVERY)
    sections, columns = lax.axis_size("layer"), lax.axis_size("tensor")
    levels = weight_hbm.shape[0]
    width = embeddings.shape[1]
    rows = embeddings.shape[0] // chunks
    tile = min(256, width)

    loads = [
        pltpu.make_async_copy(weight_hbm.at[level], weight.at[level], weight_sem.at[level])
        for level in range(levels)
    ]
    for load in loads:
        load.start()

    barrier = pltpu.get_barrier_semaphore()

    def greet(row, column):
        pl.semaphore_signal(barrier, inc=1, device_id=(dp, row, column), device_id_type=MESH)

    for column in range(columns):
        pl.when(column != me)(lambda column=column: greet(section, column))
        pl.when(section > 0)(lambda column=column: greet(section - 1, column))
        pl.when(section + 1 < sections)(lambda column=column: greet(section + 1, column))
    edges = jnp.where(section > 0, 1, 0) + jnp.where(section + 1 < sections, 1, 0)
    pl.semaphore_wait(barrier, columns - 1 + columns * edges)

    def copy(stage, chunk, source, column):
        level, row = (stage, section) if stage < levels else (0, section + 1)
        return pltpu.make_async_remote_copy(
            src_ref=source,
            dst_ref=hidden.at[level, chunk, me],
            send_sem=send_sem.at[stage, chunk, column],
            recv_sem=recv_sem.at[level, chunk, me],
            device_id=(dp, row, column),
            device_id_type=MESH,
        )

    def source_of(stage, chunk):
        return hidden.at[stage, chunk, me] if stage < levels else outbox.at[chunk]

    def sends(stage, chunk, action):
        for column in range(columns):
            if stage == 0:
                wanted = (section == 0) & (column != me)
            elif stage < levels:
                wanted = column != me
            else:
                wanted = section + 1 < sections
            pl.when(wanted)(lambda column=column: action(copy(stage, chunk, source_of(stage, chunk), column)))

    def arrivals(level, chunk):
        for column in range(columns):
            wanted = column != me
            if level == 0:
                wanted = wanted | (section > 0)

            @pl.when(wanted)
            def _():
                pltpu.make_async_remote_copy(
                    src_ref=hidden.at[level, chunk, column],
                    dst_ref=hidden.at[level, chunk, column],
                    send_sem=send_sem.at[level, chunk, column],
                    recv_sem=recv_sem.at[level, chunk, column],
                    device_id=(dp, section, column),
                    device_id_type=MESH,
                ).wait_recv()

    for chunk in range(chunks):

        @pl.when(section == 0)
        def _():
            hidden[0, chunk, me] = embeddings[chunk * rows : (chunk + 1) * rows, :]

        sends(0, chunk, lambda one: one.start())

    for level in range(levels):
        for chunk in range(chunks):
            arrivals(level, chunk)
            total = jnp.zeros((rows, 1), jnp.float32)
            for column in range(columns):
                widened = hidden[level, chunk, column].astype(jnp.float32)
                total = total + jnp.sum(widened * widened, axis=-1, keepdims=True)
            inverse = lax.rsqrt(total / (columns * width) + 1e-05)
            for column in range(columns):
                widened = hidden[level, chunk, column].astype(jnp.float32)
                records[level, chunk, :, column * width : (column + 1) * width] = (widened * inverse).astype(HALF)
            if chunk == 0:
                loads[level].wait()

            def multiply(part, _):
                place = pl.ds(pl.multiple_of(part * tile, tile), tile)
                update = jnp.dot(
                    records[level, chunk], weight[level, :, place], preferred_element_type=jnp.float32
                )
                fresh = (hidden[level, chunk, me, :, place].astype(jnp.float32) + update).astype(HALF)
                if level + 1 < levels:
                    hidden[level + 1, chunk, me, :, place] = fresh
                else:
                    outbox[chunk, :, place] = fresh
                return 0

            lax.fori_loop(0, width // tile, multiply, 0)
            sends(level + 1, chunk, lambda one: one.start())
    for stage in range(levels + 1):
        for chunk in range(chunks):
            sends(stage, chunk, lambda one: one.wait_send())


def run_layers(embeddings, layer_weight):
    levels, full, width = layer_weight.shape
    tokens = embeddings.shape[0]
    columns = lax.axis_size("tensor")
    rows = tokens // CHUNKS
    records = pl.pallas_call(
        functools.partial(layers_kernel, CHUNKS),
        out_shape=jax.ShapeDtypeStruct((levels, CHUNKS, rows, full), HALF),
        in_specs=[pl.BlockSpec(memory_space=pltpu.VMEM), pl.BlockSpec(memory_space=pl.ANY)],
        out_specs=pl.BlockSpec(memory_space=pltpu.VMEM),
        scratch_shapes=[
            pltpu.VMEM((levels, CHUNKS, columns, rows, width), HALF),
            pltpu.VMEM((CHUNKS, rows, width), HALF),
            pltpu.VMEM((levels, full, width), HALF),
            pltpu.SemaphoreType.DMA((levels + 1, CHUNKS, columns)),
            pltpu.SemaphoreType.DMA((levels, CHUNKS, columns)),
            pltpu.SemaphoreType.DMA((levels,)),
        ],
        compiler_params=pltpu.CompilerParams(
            collective_id=0, has_side_effects=True, vmem_limit_bytes=40 * 1024 * 1024
        ),
        cost_estimate=pl.CostEstimate(
            flops=2 * tokens * full * width * levels * 40,
            bytes_accessed=layer_weight.size * 2 * 20,
            transcendentals=0,
        ),
    )(embeddings, layer_weight)
    return records.reshape(levels * tokens, full)


def transposed_block(block):
    row_groups = lax.axis_size("dp") * lax.axis_size("layer")
    columns = lax.axis_size("tensor")
    share = row_groups // columns
    side = block.shape[0]
    own = lax.axis_index(ROWS) % share
    result = jnp.zeros_like(block)
    for turn in range(share):
        pairs = []
        for i in range(row_groups):
            for t in range(columns):
                part = (i + turn) % share
                pairs.append((i * columns + t, (share * t + part) * columns + i // share))
        piece = lax.dynamic_slice_in_dim(block, ((own + turn) % share) * side, side, 1)
        got = lax.ppermute(piece, EVERY, pairs)
        place = (own + share - turn) % share
        result = lax.dynamic_update_slice_in_dim(result, got.T, place * side, 1)
    return result


def shards(embeddings, layer_weight, rotation):
    full_width = layer_weight.shape[1]
    root_width = math.sqrt(full_width)
    rotated = rotation / root_width
    panel, panel_rest = (lax.all_gather(part, ROWS, axis=0, tiled=True) for part in split(rotated))
    activations = run_layers(embeddings, layer_weight)
    projected = product(activations, panel, 1, 0) + product(activations, panel_rest, 1, 0)
    cubed = projected * projected * projected
    partial = product(activations, cubed, 0, 0).astype(HALF)
    summed = lax.psum_scatter(partial, ROWS, scatter_dimension=0, tiled=True)
    gradient = summed.astype(jnp.float32) / (embeddings.shape[0] * lax.axis_size("dp"))
    cross_part = (product(gradient, panel, 1, 1) + product(gradient, panel_rest, 1, 1)).astype(HALF)
    cross = lax.psum_scatter(cross_part, "tensor", scatter_dimension=1, tiled=True)
    skew = cross.astype(jnp.float32) - transposed_block(cross).astype(jnp.float32)
    skew_rows = lax.all_gather(skew.astype(HALF), "tensor", axis=1, tiled=True)
    first_product = product(skew_rows, panel, 1, 0)
    product_panel = lax.all_gather(first_product.astype(HALF), ROWS, axis=0, tiled=True)
    square_total = lax.psum(jnp.sum(skew * skew), EVERY)
    mean_square = square_total / (full_width * full_width)
    step_size = 0.5 / jnp.sqrt(full_width * (mean_square + 1e-06))
    second_product = product(skew_rows, product_panel, 1, 0)
    refined = rotated - step_size * first_product + (0.5 * step_size * step_size) * second_product
    return root_width * refined


def solution(mesh):
    return jax.shard_map(
        shards,
        mesh=mesh,
        in_specs=(P("dp", "tensor"), P("layer", None, "tensor"), P(("dp", "layer"), "tensor")),
        out_specs=P(("dp", "layer"), "tensor"),
        check_vma=False,
    )
```

```python
import functools
import math

import jax
import jax.numpy as jnp
from jax import lax
from jax.experimental import pallas as pl
from jax.experimental.pallas import tpu as pltpu
from jax.sharding import PartitionSpec as P

ROWS = ("dp", "layer")
EVERY = ("dp", "layer", "tensor")
HALF = jnp.bfloat16
CHUNKS = 2
MESH = pl.DeviceIdType.MESH


def product(left, right, left_dim, right_dim):
    dims = (((left_dim,), (right_dim,)), ((), ()))
    return lax.dot_general(left.astype(HALF), right.astype(HALF), dims, preferred_element_type=jnp.float32)


def split(value):
    head = lax.reduce_precision(value, 8, 7)
    return head.astype(HALF), (value - head).astype(HALF)


def layers_kernel(chunks, embeddings, weight_hbm, records, hidden, outbox, weight, send_sem, recv_sem, weight_sem):
    dp, section, me = (lax.axis_index(name) for name in EVERY)
    sections, columns = lax.axis_size("layer"), lax.axis_size("tensor")
    levels = weight_hbm.shape[0]
    width = embeddings.shape[1]
    rows = embeddings.shape[0] // chunks
    tile = min(256, width)

    loads = [
        pltpu.make_async_copy(weight_hbm.at[level], weight.at[level], weight_sem.at[level])
        for level in range(levels)
    ]
    for load in loads:
        load.start()

    barrier = pltpu.get_barrier_semaphore()

    def greet(row, column):
        pl.semaphore_signal(barrier, inc=1, device_id=(dp, row, column), device_id_type=MESH)

    for column in range(columns):
        pl.when(column != me)(lambda column=column: greet(section, column))
        pl.when(section > 0)(lambda column=column: greet(section - 1, column))
        pl.when(section + 1 < sections)(lambda column=column: greet(section + 1, column))
    edges = jnp.where(section > 0, 1, 0) + jnp.where(section + 1 < sections, 1, 0)
    pl.semaphore_wait(barrier, columns - 1 + columns * edges)

    def copy(stage, chunk, source, column):
        level, row = (stage, section) if stage < levels else (0, section + 1)
        return pltpu.make_async_remote_copy(
            src_ref=source,
            dst_ref=hidden.at[level, chunk, me],
            send_sem=send_sem.at[stage, chunk, column],
            recv_sem=recv_sem.at[level, chunk, me],
            device_id=(dp, row, column),
            device_id_type=MESH,
        )

    def source_of(stage, chunk):
        return hidden.at[stage, chunk, me] if stage < levels else outbox.at[chunk]

    def sends(stage, chunk, action):
        for column in range(columns):
            if stage == 0:
                wanted = (section == 0) & (column != me)
            elif stage < levels:
                wanted = column != me
            else:
                wanted = section + 1 < sections
            pl.when(wanted)(lambda column=column: action(copy(stage, chunk, source_of(stage, chunk), column)))

    def arrivals(level, chunk):
        for column in range(columns):
            wanted = column != me
            if level == 0:
                wanted = wanted | (section > 0)

            @pl.when(wanted)
            def _():
                pltpu.make_async_remote_copy(
                    src_ref=hidden.at[level, chunk, column],
                    dst_ref=hidden.at[level, chunk, column],
                    send_sem=send_sem.at[level, chunk, column],
                    recv_sem=recv_sem.at[level, chunk, column],
                    device_id=(dp, section, column),
                    device_id_type=MESH,
                ).wait_recv()

    for chunk in range(chunks):

        @pl.when(section == 0)
        def _():
            hidden[0, chunk, me] = embeddings[chunk * rows : (chunk + 1) * rows, :]

        sends(0, chunk, lambda one: one.start())

    for level in range(levels):
        for chunk in range(chunks):
            arrivals(level, chunk)
            total = jnp.zeros((rows, 1), jnp.float32)
            for column in range(columns):
                widened = hidden[level, chunk, column].astype(jnp.float32)
                total = total + jnp.sum(widened * widened, axis=-1, keepdims=True)
            inverse = lax.rsqrt(total / (columns * width) + 1e-05)
            for column in range(columns):
                widened = hidden[level, chunk, column].astype(jnp.float32)
                records[level, chunk, :, column * width : (column + 1) * width] = (widened * inverse).astype(HALF)
            if chunk == 0:
                loads[level].wait()

            def multiply(part, _):
                place = pl.ds(pl.multiple_of(part * tile, tile), tile)
                update = jnp.dot(
                    records[level, chunk], weight[level, :, place], preferred_element_type=jnp.float32
                )
                fresh = (hidden[level, chunk, me, :, place].astype(jnp.float32) + update).astype(HALF)
                if level + 1 < levels:
                    hidden[level + 1, chunk, me, :, place] = fresh
                else:
                    outbox[chunk, :, place] = fresh
                return 0

            lax.fori_loop(0, width // tile, multiply, 0)
            sends(level + 1, chunk, lambda one: one.start())
    for stage in range(levels + 1):
        for chunk in range(chunks):
            sends(stage, chunk, lambda one: one.wait_send())


def run_layers(embeddings, layer_weight):
    levels, full, width = layer_weight.shape
    tokens = embeddings.shape[0]
    columns = lax.axis_size("tensor")
    rows = tokens // CHUNKS
    records = pl.pallas_call(
        functools.partial(layers_kernel, CHUNKS),
        out_shape=jax.ShapeDtypeStruct((levels, CHUNKS, rows, full), HALF),
        in_specs=[pl.BlockSpec(memory_space=pltpu.VMEM), pl.BlockSpec(memory_space=pl.ANY)],
        out_specs=pl.BlockSpec(memory_space=pltpu.VMEM),
        scratch_shapes=[
            pltpu.VMEM((levels, CHUNKS, columns, rows, width), HALF),
            pltpu.VMEM((CHUNKS, rows, width), HALF),
            pltpu.VMEM((levels, full, width), HALF),
            pltpu.SemaphoreType.DMA((levels + 1, CHUNKS, columns)),
            pltpu.SemaphoreType.DMA((levels, CHUNKS, columns)),
            pltpu.SemaphoreType.DMA((levels,)),
        ],
        compiler_params=pltpu.CompilerParams(
            collective_id=0, has_side_effects=True, vmem_limit_bytes=40 * 1024 * 1024
        ),
        cost_estimate=pl.CostEstimate(
            flops=2 * tokens * full * width * levels * 40,
            bytes_accessed=layer_weight.size * 2 * 20,
            transcendentals=0,
        ),
    )(embeddings, layer_weight)
    return records.reshape(levels * tokens, full)


def transposed_block(block):
    row_groups = lax.axis_size("dp") * lax.axis_size("layer")
    columns = lax.axis_size("tensor")
    share = row_groups // columns
    side = block.shape[0]
    own = lax.axis_index(ROWS) % share
    result = jnp.zeros_like(block)
    for turn in range(share):
        pairs = []
        for i in range(row_groups):
            for t in range(columns):
                part = (i + turn) % share
                pairs.append((i * columns + t, (share * t + part) * columns + i // share))
        piece = lax.dynamic_slice_in_dim(block, ((own + turn) % share) * side, side, 1)
        got = lax.ppermute(piece, EVERY, pairs)
        place = (own + share - turn) % share
        result = lax.dynamic_update_slice_in_dim(result, got.T, place * side, 1)
    return result


def shards(embeddings, layer_weight, rotation):
    full_width = layer_weight.shape[1]
    root_width = math.sqrt(full_width)
    rotated = rotation / root_width
    panel, panel_rest = (lax.all_gather(part, ROWS, axis=0, tiled=True) for part in split(rotated))
    activations = run_layers(embeddings, layer_weight)
    projected = product(activations, panel, 1, 0) + product(activations, panel_rest, 1, 0)
    cubed = projected * projected * projected
    groups = lax.axis_size("dp") * lax.axis_size("layer")
    grouped = activations.reshape(activations.shape[0], groups, 2, full_width // groups // 2)
    crosses = []
    for half in range(2):
        chosen = grouped[:, :, half].reshape(activations.shape[0], full_width // 2)
        partial = product(chosen, cubed, 0, 0).astype(HALF)
        summed = lax.psum_scatter(partial, ROWS, scatter_dimension=0, tiled=True)
        gradient = summed.astype(jnp.float32) / (embeddings.shape[0] * lax.axis_size("dp"))
        cross_part = (product(gradient, panel, 1, 1) + product(gradient, panel_rest, 1, 1)).astype(HALF)
        crosses.append(lax.psum_scatter(cross_part, "tensor", scatter_dimension=1, tiled=True))
    cross = jnp.concatenate(crosses, axis=0)
    skew = cross.astype(jnp.float32) - transposed_block(cross).astype(jnp.float32)
    skew_rows = lax.all_gather(skew.astype(HALF), "tensor", axis=1, tiled=True)
    first_product = product(skew_rows, panel, 1, 0)
    product_panel = lax.all_gather(first_product.astype(HALF), ROWS, axis=0, tiled=True)
    square_total = lax.psum(jnp.sum(skew * skew), EVERY)
    mean_square = square_total / (full_width * full_width)
    step_size = 0.5 / jnp.sqrt(full_width * (mean_square + 1e-06))
    second_product = product(skew_rows, product_panel, 1, 0)
    refined = rotated - step_size * first_product + (0.5 * step_size * step_size) * second_product
    return root_width * refined


def solution(mesh):
    return jax.shard_map(
        shards,
        mesh=mesh,
        in_specs=(P("dp", "tensor"), P("layer", None, "tensor"), P(("dp", "layer"), "tensor")),
        out_specs=P(("dp", "layer"), "tensor"),
        check_vma=False,
    )
```

```python
import functools
import math

import jax
import jax.numpy as jnp
from jax import lax
from jax.experimental import pallas as pl
from jax.experimental.pallas import tpu as pltpu
from jax.sharding import PartitionSpec as P

ROWS = ("dp", "layer")
EVERY = ("dp", "layer", "tensor")
HALF = jnp.bfloat16
CHUNKS = 2
MESH = pl.DeviceIdType.MESH


def product(left, right, left_dim, right_dim):
    dims = (((left_dim,), (right_dim,)), ((), ()))
    return lax.dot_general(left.astype(HALF), right.astype(HALF), dims, preferred_element_type=jnp.float32)


def split(value):
    head = lax.reduce_precision(value, 8, 7)
    return head.astype(HALF), (value - head).astype(HALF)


def layers_kernel(chunks, embeddings, weight_hbm, records, hidden, outbox, weight, send_sem, recv_sem, weight_sem):
    dp, section, me = (lax.axis_index(name) for name in EVERY)
    sections, columns = lax.axis_size("layer"), lax.axis_size("tensor")
    levels = weight_hbm.shape[0]
    width = embeddings.shape[1]
    rows = embeddings.shape[0] // chunks
    tile = min(256, width)

    loads = [
        pltpu.make_async_copy(weight_hbm.at[level], weight.at[level], weight_sem.at[level])
        for level in range(levels)
    ]
    for load in loads:
        load.start()

    barrier = pltpu.get_barrier_semaphore()

    def greet(row, column):
        pl.semaphore_signal(barrier, inc=1, device_id=(dp, row, column), device_id_type=MESH)

    for column in range(columns):
        pl.when(column != me)(lambda column=column: greet(section, column))
        pl.when(section > 0)(lambda column=column: greet(section - 1, column))
        pl.when(section + 1 < sections)(lambda column=column: greet(section + 1, column))
    edges = jnp.where(section > 0, 1, 0) + jnp.where(section + 1 < sections, 1, 0)
    pl.semaphore_wait(barrier, columns - 1 + columns * edges)

    def copy(stage, chunk, source, column):
        level, row = (stage, section) if stage < levels else (0, section + 1)
        return pltpu.make_async_remote_copy(
            src_ref=source,
            dst_ref=hidden.at[level, chunk, me],
            send_sem=send_sem.at[stage, chunk, column],
            recv_sem=recv_sem.at[level, chunk, me],
            device_id=(dp, row, column),
            device_id_type=MESH,
        )

    def source_of(stage, chunk):
        return hidden.at[stage, chunk, me] if stage < levels else outbox.at[chunk]

    def sends(stage, chunk, action):
        for column in range(columns):
            if stage == 0:
                wanted = (section == 0) & (column != me)
            elif stage < levels:
                wanted = column != me
            else:
                wanted = section + 1 < sections
            pl.when(wanted)(lambda column=column: action(copy(stage, chunk, source_of(stage, chunk), column)))

    def arrivals(level, chunk):
        for column in range(columns):
            wanted = column != me
            if level == 0:
                wanted = wanted | (section > 0)

            @pl.when(wanted)
            def _():
                pltpu.make_async_remote_copy(
                    src_ref=hidden.at[level, chunk, column],
                    dst_ref=hidden.at[level, chunk, column],
                    send_sem=send_sem.at[level, chunk, column],
                    recv_sem=recv_sem.at[level, chunk, column],
                    device_id=(dp, section, column),
                    device_id_type=MESH,
                ).wait_recv()

    for chunk in range(chunks):

        @pl.when(section == 0)
        def _():
            hidden[0, chunk, me] = embeddings[chunk * rows : (chunk + 1) * rows, :]

        sends(0, chunk, lambda one: one.start())

    for level in range(levels):
        for chunk in range(chunks):
            arrivals(level, chunk)
            total = jnp.zeros((rows, 1), jnp.float32)
            for column in range(columns):
                widened = hidden[level, chunk, column].astype(jnp.float32)
                total = total + jnp.sum(widened * widened, axis=-1, keepdims=True)
            inverse = lax.rsqrt(total / (columns * width) + 1e-05)
            for column in range(columns):
                widened = hidden[level, chunk, column].astype(jnp.float32)
                records[level, chunk, :, column * width : (column + 1) * width] = (widened * inverse).astype(HALF)
            if chunk == 0:
                loads[level].wait()

            def multiply(part, _):
                place = pl.ds(pl.multiple_of(part * tile, tile), tile)
                update = jnp.dot(
                    records[level, chunk], weight[level, :, place], preferred_element_type=jnp.float32
                )
                fresh = (hidden[level, chunk, me, :, place].astype(jnp.float32) + update).astype(HALF)
                if level + 1 < levels:
                    hidden[level + 1, chunk, me, :, place] = fresh
                else:
                    outbox[chunk, :, place] = fresh
                return 0

            lax.fori_loop(0, width // tile, multiply, 0)
            sends(level + 1, chunk, lambda one: one.start())
    for stage in range(levels + 1):
        for chunk in range(chunks):
            sends(stage, chunk, lambda one: one.wait_send())


def run_layers(embeddings, layer_weight):
    levels, full, width = layer_weight.shape
    tokens = embeddings.shape[0]
    columns = lax.axis_size("tensor")
    rows = tokens // CHUNKS
    records = pl.pallas_call(
        functools.partial(layers_kernel, CHUNKS),
        out_shape=jax.ShapeDtypeStruct((levels, CHUNKS, rows, full), HALF),
        in_specs=[pl.BlockSpec(memory_space=pltpu.VMEM), pl.BlockSpec(memory_space=pl.ANY)],
        out_specs=pl.BlockSpec(memory_space=pltpu.VMEM),
        scratch_shapes=[
            pltpu.VMEM((levels, CHUNKS, columns, rows, width), HALF),
            pltpu.VMEM((CHUNKS, rows, width), HALF),
            pltpu.VMEM((levels, full, width), HALF),
            pltpu.SemaphoreType.DMA((levels + 1, CHUNKS, columns)),
            pltpu.SemaphoreType.DMA((levels, CHUNKS, columns)),
            pltpu.SemaphoreType.DMA((levels,)),
        ],
        compiler_params=pltpu.CompilerParams(
            collective_id=0, has_side_effects=True, vmem_limit_bytes=40 * 1024 * 1024
        ),
        cost_estimate=pl.CostEstimate(
            flops=2 * tokens * full * width * levels * 40,
            bytes_accessed=layer_weight.size * 2 * 20,
            transcendentals=0,
        ),
    )(embeddings, layer_weight)
    return records.reshape(levels * tokens, full)


def transposed_block(block):
    row_groups = lax.axis_size("dp") * lax.axis_size("layer")
    columns = lax.axis_size("tensor")
    share = row_groups // columns
    side = block.shape[0]
    own = lax.axis_index(ROWS) % share
    result = jnp.zeros_like(block)
    for turn in range(share):
        pairs = []
        for i in range(row_groups):
            for t in range(columns):
                part = (i + turn) % share
                pairs.append((i * columns + t, (share * t + part) * columns + i // share))
        piece = lax.dynamic_slice_in_dim(block, ((own + turn) % share) * side, side, 1)
        got = lax.ppermute(piece, EVERY, pairs)
        place = (own + share - turn) % share
        result = lax.dynamic_update_slice_in_dim(result, got.T, place * side, 1)
    return result


def gathered_columns(block):
    count, me, width = lax.axis_size("tensor"), lax.axis_index("tensor"), block.shape[1]
    result = jnp.zeros((block.shape[0], count * width), block.dtype)
    for turn in range(count):
        got = block
        if turn:
            got = lax.ppermute(block, "tensor", [(t, (t + turn) % count) for t in range(count)])
        result = lax.dynamic_update_slice_in_dim(result, got, ((me + count - turn) % count) * width, 1)
    return result


def shards(embeddings, layer_weight, rotation):
    full_width = layer_weight.shape[1]
    root_width = math.sqrt(full_width)
    rotated = rotation / root_width
    panel, panel_rest = (lax.all_gather(part, ROWS, axis=0, tiled=True) for part in split(rotated))
    activations = run_layers(embeddings, layer_weight)
    projected = product(activations, panel, 1, 0) + product(activations, panel_rest, 1, 0)
    cubed = projected * projected * projected
    partial = product(activations, cubed, 0, 0).astype(HALF)
    summed = lax.psum_scatter(partial, ROWS, scatter_dimension=0, tiled=True)
    gradient = summed.astype(jnp.float32) / (embeddings.shape[0] * lax.axis_size("dp"))
    cross_part = (product(gradient, panel, 1, 1) + product(gradient, panel_rest, 1, 1)).astype(HALF)
    cross = lax.psum_scatter(cross_part, "tensor", scatter_dimension=1, tiled=True)
    skew = cross.astype(jnp.float32) - transposed_block(cross).astype(jnp.float32)
    skew_rows = gathered_columns(skew.astype(HALF))
    first_product = product(skew_rows, panel, 1, 0)
    product_panel = lax.all_gather(first_product.astype(HALF), ROWS, axis=0, tiled=True)
    square_total = lax.psum(jnp.sum(skew * skew), EVERY)
    mean_square = square_total / (full_width * full_width)
    step_size = 0.5 / jnp.sqrt(full_width * (mean_square + 1e-06))
    second_product = product(skew_rows, product_panel, 1, 0)
    refined = rotated - step_size * first_product + (0.5 * step_size * step_size) * second_product
    return root_width * refined


def solution(mesh):
    return jax.shard_map(
        shards,
        mesh=mesh,
        in_specs=(P("dp", "tensor"), P("layer", None, "tensor"), P(("dp", "layer"), "tensor")),
        out_specs=P(("dp", "layer"), "tensor"),
        check_vma=False,
    )
```
